32 devices in a mesh: seq: 8 (over z, x), head: 4 (over y, core).
Axes of the slice: x: 2, y: 2, z: 4, core: 2. Of those that a mesh axis runs over, the one named last changes fastest.
Arguments:
- h_in: float32 [2048, 1024], P('seq', 'head'), may hold values from -6 to 6
- norm_gain: float32 [2, 1024], P(None, 'head'), may hold values from 0.5 to 1.5
- w_z: bfloat16 [2, 1024, 2048], P(None, None, 'head'), may hold values from -0.1875 to 0.1875
- w_x: bfloat16 [2, 1024, 2048], P(None, None, 'head'), may hold values from -0.1875 to 0.1875
- w_bc: bfloat16 [2, 1024, 256], replicated, may hold values from -0.1875 to 0.1875
- w_dt: bfloat16 [2, 1024, 32], P(None, None, 'head'), may hold values from -0.1875 to 0.1875
- conv_x_w: float32 [2, 4, 2048], P(None, None, 'head'), may hold values from -3 to 3
- conv_x_b: float32 [2, 2048], P(None, 'head'), may hold values from -0.5 to 0.5
- conv_bc_w: float32 [2, 4, 256], replicated, may hold values from -3 to 3
- conv_bc_b: float32 [2, 256], replicated, may hold values from -0.5 to 0.5
- dt_bias: float32 [2, 32], P(None, 'head'), may hold values from -4 to -1
- a_log: float32 [2, 32], P(None, 'head'), may hold values from -10 to -1
- skip: float32 [2, 32], P(None, 'head'), may hold values from 0.5 to 1.5
- gate_gain: float32 [2, 2048], P(None, 'head'), may hold values from 0.5 to 1.5
- w_out: bfloat16 [2, 2048, 1024], P(None, 'head'), may hold values from -0.125 to 0.125
- d_out: float32 [2048, 1024], P('seq', 'head'), may hold values from -6 to 6
Outputs:
- h_out: float32 [2048, 1024], P('seq', 'head')
- d_h: float32 [2048, 1024], P('seq', 'head')
- d_norm_gain: float32 [2, 1024], P(None, 'head')
- d_w_z: float32 [2, 1024, 2048], P(None, 'seq', 'head')
- d_w_x: float32 [2, 1024, 2048], P(None, 'seq', 'head')
- d_w_bc: float32 [2, 1024, 256], replicated
- d_w_dt: float32 [2, 1024, 32], P(None, 'seq', 'head')
- d_conv_x_w: float32 [2, 4, 2048], P(None, None, 'head')
- d_conv_x_b: float32 [2, 2048], P(None, 'head')
- d_conv_bc_w: float32 [2, 4, 256], replicated
- d_conv_bc_b: float32 [2, 256], replicated
- d_dt_bias: float32 [2, 32], P(None, 'head')
- d_a_log: float32 [2, 32], P(None, 'head')
- d_skip: float32 [2, 32], P(None, 'head')
- d_gate_gain: float32 [2, 2048], P(None, 'head')
- d_w_out: float32 [2, 2048, 1024], P(None, 'head', 'seq')
The draws below stay inside these ranges and needn't reach their ends.
All inputs are finite; a program needn't handle non-finite values.
Results may differ from the reference program's by a relative error of at most 0.014.
The reference program's roundings to bfloat16 on the way (of `normed`, `scaled`, `grad_b` and `d_gate_b`) count: a program that leaves them out, or rounds other values in their place, can miss the bound.
Values may be sent and summed in bfloat16 or wider, within the bound.
A program may use at most 128 MiB of HBM per device.

```python
import jax
import jax.numpy as jnp
from jax import lax

D = 1024
HEADS = 32
HEAD_DIM = 64
STATE = 128
CONV = 4
SPAN = 256
LAYERS = 2
DI = 2048
LENGTH = 2048


def levels(stream_key, shape, pieces, low, top_value):
    level = 1.0
    for axis_at, shards_of in pieces:
        heights = jax.random.uniform(jax.random.fold_in(jax.random.fold_in(stream_key, 6), axis_at), (shards_of,), jnp.float32, low / len(pieces), top_value / len(pieces))
        level = level * jnp.repeat(jnp.exp(heights), shape[axis_at] // shards_of).reshape((-1,) + (1,) * (len(shape) - 1 - axis_at))
    return level


def normal_values(own_key, shape, scale, most, shards=(), dtype=jnp.bfloat16):
    values = scale * jax.random.normal(own_key, shape, jnp.float32)
    if shards:
        values = values * levels(own_key, shape, shards, -0.22, 0.18)
    return jnp.clip(values, -most, most).astype(dtype)


def setup_inputs(seed: int = 0) -> dict:
    keys = jax.random.split(jax.random.key(seed), 17)
    return {
        "h_in": normal_values(keys[0], (LENGTH, D), 1.0, 6.0, ((0, 8), (1, 4)), jnp.float32),
        "norm_gain": jnp.clip(1.0 + 0.1 * jax.random.normal(keys[1], (LAYERS, D), jnp.float32), 0.5, 1.5),
        "w_z": normal_values(keys[2], (LAYERS, D, DI), D ** -0.5, 0.1875, ((2, 4),)),
        "w_x": normal_values(keys[3], (LAYERS, D, DI), D ** -0.5, 0.1875, ((2, 4),)),
        "w_bc": normal_values(keys[4], (LAYERS, D, 2 * STATE), D ** -0.5, 0.1875),
        "w_dt": normal_values(keys[5], (LAYERS, D, HEADS), D ** -0.5, 0.1875, ((2, 4),)),
        "conv_x_w": normal_values(keys[6], (LAYERS, CONV, DI), CONV ** -0.5, 3.0, ((2, 4),), jnp.float32),
        "conv_x_b": jnp.clip(jax.random.uniform(keys[7], (LAYERS, DI), jnp.float32, -0.5, 0.5) * levels(keys[7], (LAYERS, DI), ((1, 4),), -0.4, 0.0), -0.5, 0.5),
        "conv_bc_w": normal_values(keys[8], (LAYERS, CONV, 2 * STATE), CONV ** -0.5, 3.0, (), jnp.float32),
        "conv_bc_b": jnp.clip(jax.random.uniform(keys[9], (LAYERS, 2 * STATE), jnp.float32, -0.5, 0.5), -0.5, 0.5),
        "dt_bias": jnp.clip(-4.0 + 3.0 * jax.random.uniform(keys[10], (LAYERS, HEADS), jnp.float32) ** levels(keys[10], (LAYERS, HEADS), ((1, 4),), -0.2, 0.2), -4.0, -1.0),
        "a_log": jnp.clip(-10.0 + 9.0 * jax.random.uniform(keys[11], (LAYERS, HEADS), jnp.float32) ** levels(keys[11], (LAYERS, HEADS), ((1, 4),), -0.2, 0.2), -10.0, -1.0),
        "skip": jnp.clip(0.5 + 1.0 * jax.random.uniform(keys[12], (LAYERS, HEADS), jnp.float32) ** levels(keys[12], (LAYERS, HEADS), ((1, 4),), -0.2, 0.2), 0.5, 1.5),
        "gate_gain": jnp.clip(1.0 + 0.1 * jax.random.normal(keys[13], (LAYERS, DI), jnp.float32), 0.5, 1.5),
        "w_out": normal_values(keys[14], (LAYERS, DI, D), DI ** -0.5, 0.125, ((1, 4),)),
        "d_out": normal_values(keys[15], (LENGTH, D), 1.0, 6.0, ((0, 8), (1, 4)), jnp.float32),
    }


epsilon = 1e-05
highest = lax.Precision.HIGHEST

def rms_scale(hidden, gain):
    factor = lax.rsqrt(lax.optimization_barrier(jnp.mean(hidden * hidden, axis=1)) + epsilon)
    return hidden * factor[:, None] * gain[None, :]

def conv_inputs(extended, dt_raw, conv_weight, conv_bias, dt_bias, a_log):
    row_count = dt_raw.shape[0]
    mixed = jnp.zeros((row_count, extended.shape[1]), jnp.float32) + conv_bias[None, :]
    for offset in range(CONV):
        mixed = mixed + conv_weight[offset][None, :] * extended[offset:offset + row_count]
    active = jax.nn.silu(mixed)
    inner = extended.shape[1] - 2 * STATE
    head_count = dt_raw.shape[1]
    values = active[:, :inner].reshape(row_count, head_count, HEAD_DIM)
    b_proj = active[:, inner:inner + STATE]
    c_proj = active[:, inner + STATE:]
    steps_dt = jax.nn.softplus(dt_raw + dt_bias[None, :])
    log_decay = -steps_dt * jnp.exp(a_log)[None, :]
    return (values, b_proj, c_proj, steps_dt, log_decay)

def block_scan(values, b_proj, c_proj, steps_dt, log_decay, initial):
    row_count, head_count = steps_dt.shape
    blocks = row_count // SPAN
    causal = (jnp.arange(SPAN)[:, None] >= jnp.arange(SPAN)[None, :])[None]

    def one_block(carried, block_data):
        block_vals, b_blk, c_blk, dt_blk, la_blk = block_data
        cumulative = jnp.cumsum(la_blk, axis=0)
        cum_heads = cumulative.T
        spread = cum_heads[:, :, None] - cum_heads[:, None, :]
        weights = jnp.where(causal, jnp.exp(jnp.where(causal, spread, 0.0)), 0.0)
        scores = jnp.dot(c_blk, b_blk.T, precision=highest)
        scaled = block_vals * dt_blk[:, :, None]
        y_diag = jnp.einsum('htu,uhp->thp', weights * scores[None], scaled, precision=highest)
        y_off = jnp.einsum('tn,hpn->thp', c_blk, carried, precision=highest) * jnp.exp(cumulative)[:, :, None]
        ending = cumulative[-1]
        tail_decay = jnp.exp(ending[None, :] - cumulative)
        updated = carried * jnp.exp(ending)[:, None, None] + jnp.einsum('uhp,un->hpn', scaled * tail_decay[:, :, None], b_blk, precision=highest)
        return (updated, y_diag + y_off)
    stacked = (values.reshape(blocks, SPAN, head_count, HEAD_DIM), b_proj.reshape(blocks, SPAN, STATE), c_proj.reshape(blocks, SPAN, STATE), steps_dt.reshape(blocks, SPAN, head_count), log_decay.reshape(blocks, SPAN, head_count))
    last_state, outputs = lax.scan(one_block, initial, stacked)
    return (outputs.reshape(row_count, head_count, HEAD_DIM), last_state)

def mixer_core(gate_in, conv_in, dt_raw, conv_weight, conv_bias, dt_bias, a_log, skip, gate_gain):
    row_count, head_count = dt_raw.shape
    extended = jnp.concatenate([jnp.zeros((CONV - 1, conv_in.shape[1]), jnp.float32), conv_in], axis=0)
    values, b_proj, c_proj, steps_dt, log_decay = conv_inputs(extended, dt_raw, conv_weight, conv_bias, dt_bias, a_log)
    scanned, last_state = block_scan(values, b_proj, c_proj, steps_dt, log_decay, jnp.zeros((head_count, HEAD_DIM, STATE), jnp.float32))
    mixed = scanned + skip[None, :, None] * values
    gated = mixed.reshape(row_count, head_count * HEAD_DIM) * jax.nn.silu(gate_in)
    factor = lax.rsqrt(lax.optimization_barrier(jnp.mean(gated * gated, axis=1)) + epsilon)
    return gated * factor[:, None] * gate_gain[None, :]

def reference(h_in, norm_gain, w_z, w_x, w_bc, w_dt, conv_x_w, conv_x_b, conv_bc_w, conv_bc_b, dt_bias, a_log, skip, gate_gain, w_out, d_out):
    hidden = h_in
    inner = w_x.shape[2]
    kept = []
    for layer_idx in range(LAYERS):
        normed_full, norm_back = jax.vjp(rms_scale, hidden, norm_gain[layer_idx])
        normed = normed_full.astype(jnp.bfloat16)
        gate_in = jnp.dot(normed, w_z[layer_idx], preferred_element_type=jnp.float32)
        x_in = jnp.dot(normed, w_x[layer_idx], preferred_element_type=jnp.float32)
        bc_in = jnp.dot(normed, w_bc[layer_idx], preferred_element_type=jnp.float32)
        dt_raw = jnp.dot(normed, w_dt[layer_idx], preferred_element_type=jnp.float32)
        conv_in = jnp.concatenate([x_in, bc_in], axis=1)
        conv_weight = jnp.concatenate([conv_x_w[layer_idx], conv_bc_w[layer_idx]], axis=1)
        conv_bias = jnp.concatenate([conv_x_b[layer_idx], conv_bc_b[layer_idx]], axis=0)
        scaled_full, core_back = jax.vjp(mixer_core, gate_in, conv_in, dt_raw, conv_weight, conv_bias, dt_bias[layer_idx], a_log[layer_idx], skip[layer_idx], gate_gain[layer_idx])
        scaled = scaled_full.astype(jnp.bfloat16)
        kept.append((normed, norm_back, core_back, scaled))
        hidden = hidden + jnp.dot(scaled, w_out[layer_idx], preferred_element_type=jnp.float32)
    h_out = hidden
    grad = d_out
    collected = [None] * LAYERS
    for layer_idx in reversed(range(LAYERS)):
        normed, norm_back, core_back, scaled = kept[layer_idx]
        grad_b = grad.astype(jnp.bfloat16)
        d_scaled = jnp.dot(grad_b, w_out[layer_idx].T, preferred_element_type=jnp.float32)
        d_wout = jnp.dot(scaled.T, grad_b, preferred_element_type=jnp.float32)
        d_gate, d_conv, d_dtraw, d_cweight, d_cbias, d_dtbias, d_alog, d_skipped, d_ggain = core_back(d_scaled)
        d_gate_b = d_gate.astype(jnp.bfloat16)
        d_x_b = d_conv[:, :inner].astype(jnp.bfloat16)
        d_shared = d_conv[:, inner:]
        d_dt_b = d_dtraw.astype(jnp.bfloat16)
        d_wz = jnp.dot(normed.T, d_gate_b, preferred_element_type=jnp.float32)
        d_wx = jnp.dot(normed.T, d_x_b, preferred_element_type=jnp.float32)
        d_wdt = jnp.dot(normed.T, d_dt_b, preferred_element_type=jnp.float32)
        d_wbc = jnp.dot(normed.astype(jnp.float32).T, d_shared, precision=highest)
        d_normed = jnp.dot(d_gate_b, w_z[layer_idx].T, preferred_element_type=jnp.float32)
        d_normed = d_normed + jnp.dot(d_x_b, w_x[layer_idx].T, preferred_element_type=jnp.float32)
        d_normed = d_normed + jnp.dot(d_dt_b, w_dt[layer_idx].T, preferred_element_type=jnp.float32)
        d_normed = d_normed + jnp.dot(d_shared, w_bc[layer_idx].astype(jnp.float32).T, precision=highest)
        d_hidden, d_ngain = norm_back(d_normed)
        grad = grad + d_hidden
        collected[layer_idx] = (d_ngain, d_wz, d_wx, d_wbc, d_wdt, d_cweight[:, :inner], d_cbias[:inner], d_cweight[:, inner:], d_cbias[inner:], d_dtbias, d_alog, d_skipped, d_ggain, d_wout)
    stacks = [jnp.stack([collected[layer_idx][member] for layer_idx in range(LAYERS)]) for member in range(14)]
    return (h_out, grad, stacks[0], stacks[1], stacks[2], stacks[3], stacks[4], stacks[5], stacks[6], stacks[7], stacks[8], stacks[9], stacks[10], stacks[11], stacks[12], stacks[13])
```

```python
import jax
import jax.numpy as jnp
from jax import lax
from jax.sharding import PartitionSpec as P

D = 1024
HEAD_DIM = 64
STATE = 128
CONV = 4
SPAN = 256
LAYERS = 2
DI = 2048


epsilon = 1e-05
highest = lax.Precision.HIGHEST


def shifted(value, axis, steps):
    count = lax.axis_size(axis)
    first, last = (max(0, -steps), min(count, count - steps))
    return lax.ppermute(value, axis, [(source, source + steps) for source in range(first, last)])


def entering_state(log_total, value, axis, backward):
    count, mine = (lax.axis_size(axis), lax.axis_index(axis))
    heads, head_dim, state = value.shape
    rows = jnp.broadcast_to(log_total[:, None], (heads, state))
    packed = jnp.concatenate([value.reshape(heads * head_dim, state), rows], axis=0)
    pieces = lax.all_gather(packed, axis)
    values = pieces[:, : heads * head_dim].reshape(count, heads, head_dim, state)
    logs = pieces[:, heads * head_dim :, 0]
    source = jnp.arange(count)[:, None]
    middle = jnp.arange(count)[None, :]
    if backward:
        between, used = ((middle < source) & (middle > mine), jnp.arange(count) > mine)
    else:
        between, used = ((middle > source) & (middle < mine), jnp.arange(count) < mine)
    total = jnp.sum(jnp.where(between[:, :, None], logs[None], 0.0), axis=1)
    weights = jnp.where(used[:, None], jnp.exp(total), 0.0)
    result = weights[0][:, None, None] * values[0]
    for place in range(1, count):
        result = result + weights[place][:, None, None] * values[place]
    return result


def conv_inputs(extended, dt_raw, conv_weight, conv_bias, dt_bias, a_log):
    row_count = dt_raw.shape[0]
    mixed = jnp.zeros((row_count, extended.shape[1]), jnp.float32) + conv_bias[None, :]
    for offset in range(CONV):
        mixed = mixed + conv_weight[offset][None, :] * extended[offset : offset + row_count]
    active = jax.nn.silu(mixed)
    inner = extended.shape[1] - 2 * STATE
    head_count = dt_raw.shape[1]
    values = active[:, :inner].reshape(row_count, head_count, HEAD_DIM)
    b_proj = active[:, inner : inner + STATE]
    c_proj = active[:, inner + STATE :]
    steps_dt = jax.nn.softplus(dt_raw + dt_bias[None, :])
    log_decay = -steps_dt * jnp.exp(a_log)[None, :]
    return (values, b_proj, c_proj, steps_dt, log_decay)


def scan_from_zero(values, b_proj, c_proj, steps_dt, log_decay):
    row_count, head_count = steps_dt.shape
    causal = (jnp.arange(row_count)[:, None] >= jnp.arange(row_count)[None, :])[None]

    def one_block(carried, block_data):
        block_vals, b_blk, c_blk, dt_blk, la_blk = block_data
        cumulative = jnp.cumsum(la_blk, axis=0)
        cum_heads = cumulative.T
        spread = cum_heads[:, :, None] - cum_heads[:, None, :]
        weights = jnp.where(causal, jnp.exp(jnp.where(causal, spread, 0.0)), 0.0)
        scores = jnp.dot(c_blk, b_blk.T, precision=highest)
        scaled = block_vals * dt_blk[:, :, None]
        y_diag = jnp.einsum("htu,uhp->thp", weights * scores[None], scaled, precision=highest)
        ending = cumulative[-1]
        tail_decay = jnp.exp(ending[None, :] - cumulative)
        updated = jnp.einsum(
            "uhp,un->hpn", scaled * tail_decay[:, :, None], b_blk, precision=highest
        )
        return (updated, y_diag)

    initial = jnp.zeros((head_count, HEAD_DIM, STATE), jnp.float32)
    last_state, outputs = one_block(initial, (values, b_proj, c_proj, steps_dt, log_decay))
    return (outputs, last_state)


def carry_term(c_proj, log_decay, entering):
    cumulative = jnp.cumsum(log_decay, axis=0)
    return (
        jnp.einsum("tn,hpn->thp", c_proj, entering, precision=highest)
        * jnp.exp(cumulative)[:, :, None]
    )


def token_sums(partial_sums):
    return lax.psum(partial_sums, "head")


def contract_first(left, right):
    return lax.dot_general(
        left, right, (((0,), (0,)), ((), ())), preferred_element_type=jnp.float32
    )


def local(
    h_in,
    norm_gain,
    w_z,
    w_x,
    w_bc,
    w_dt,
    conv_x_w,
    conv_x_b,
    conv_bc_w,
    conv_bc_b,
    dt_bias,
    a_log,
    skip,
    gate_gain,
    w_out,
    d_out,
):
    row_count = h_in.shape[0]
    inner = w_x.shape[2]
    head_count = w_dt.shape[2]
    hidden = h_in
    kept = []
    all_gain = lax.all_gather(norm_gain, "head", axis=1, tiled=True)
    for layer_idx in range(LAYERS):
        full_hidden = lax.all_gather(hidden, "head", axis=1, tiled=True)
        full_gain = all_gain[layer_idx]
        factor = lax.rsqrt(jnp.mean(full_hidden * full_hidden, axis=1) + epsilon)
        normed = (full_hidden * factor[:, None] * full_gain[None, :]).astype(jnp.bfloat16)
        gate_in = jnp.dot(normed, w_z[layer_idx], preferred_element_type=jnp.float32)
        x_in = jnp.dot(normed, w_x[layer_idx], preferred_element_type=jnp.float32)
        bc_in = jnp.dot(normed, w_bc[layer_idx], preferred_element_type=jnp.float32)
        dt_raw = jnp.dot(normed, w_dt[layer_idx], preferred_element_type=jnp.float32)
        conv_in = jnp.concatenate([x_in, bc_in], axis=1)
        before = shifted(conv_in[row_count - (CONV - 1) :], "seq", 1)
        extended = jnp.concatenate([before, conv_in], axis=0)
        conv_weight = jnp.concatenate([conv_x_w[layer_idx], conv_bc_w[layer_idx]], axis=1)
        conv_bias = jnp.concatenate([conv_x_b[layer_idx], conv_bc_b[layer_idx]], axis=0)
        inputs, input_back = jax.vjp(
            conv_inputs,
            extended,
            dt_raw,
            conv_weight,
            conv_bias,
            dt_bias[layer_idx],
            a_log[layer_idx],
        )
        values, b_proj, c_proj, steps_dt, log_decay = inputs
        local_part, block_back = jax.vjp(
            scan_from_zero, values, b_proj, c_proj, steps_dt, log_decay
        )
        scanned, leaving = local_part
        log_total = jnp.sum(log_decay, axis=0)
        decays = jnp.exp(log_total)
        entering = entering_state(log_total, leaving, "seq", False)
        carried_part, carry_back = jax.vjp(carry_term, c_proj, log_decay, entering)
        mixed = scanned + carried_part + skip[layer_idx][None, :, None] * values
        gate_act = jax.nn.silu(gate_in)
        gated = mixed.reshape(row_count, inner) * gate_act
        gate_factor = lax.rsqrt(token_sums(jnp.sum(gated * gated, axis=1)) / DI + epsilon)
        scaled = (gated * gate_factor[:, None] * gate_gain[layer_idx][None, :]).astype(jnp.bfloat16)
        out_weight = w_out[layer_idx]
        summed = lax.psum_scatter(
            contract_first(out_weight, scaled.T), "head", scatter_dimension=0, tiled=True
        )
        kept.append(
            (
                hidden,
                factor,
                normed,
                gate_in,
                gate_act,
                gated,
                gate_factor,
                scaled,
                mixed,
                values,
                decays,
                log_total,
                entering,
                input_back,
                block_back,
                carry_back,
            )
        )
        hidden = hidden + summed.T
    grad = d_out
    collected = [None] * LAYERS
    for layer_idx in reversed(range(LAYERS)):
        (
            layer_input,
            factor,
            normed,
            gate_in,
            gate_act,
            gated,
            gate_factor,
            scaled,
            mixed,
            values,
            decays,
            log_total,
            entering,
            input_back,
            block_back,
            carry_back,
        ) = kept[layer_idx]
        grad_b = grad.astype(jnp.bfloat16)
        out_weight = w_out[layer_idx]
        grad_cols = lax.all_gather(grad_b, "head", axis=1, tiled=True)
        d_part = lax.dot_general(
            grad_cols, out_weight, (((1,), (1,)), ((), ())), preferred_element_type=jnp.float32
        )
        d_cols = contract_first(scaled, grad_cols)
        normalized = gated * gate_factor[:, None]
        d_ggain = jnp.sum(d_part * normalized, axis=0)
        d_norm_in = d_part * gate_gain[layer_idx][None, :]
        along = token_sums(jnp.sum(d_norm_in * normalized, axis=1)) / DI
        d_gated = gate_factor[:, None] * (d_norm_in - normalized * along[:, None])
        sigma = jax.nn.sigmoid(gate_in)
        d_gate = d_gated * mixed.reshape(row_count, inner) * sigma * (1.0 + gate_in * (1.0 - sigma))
        d_mixed = (d_gated * gate_act).reshape(row_count, head_count, HEAD_DIM)
        d_skipped = jnp.sum(d_mixed * values, axis=(0, 2))
        d_c_carry, d_la_carry, d_entering = carry_back(d_mixed)
        leaving_grad = entering_state(log_total, d_entering, "seq", True)
        d_decays = jnp.sum(leaving_grad * entering, axis=(1, 2)) * decays
        d_values, d_b_proj, d_c_local, d_steps, d_la_local = block_back((d_mixed, leaving_grad))
        d_values = d_values + skip[layer_idx][None, :, None] * d_mixed
        d_inputs = (
            d_values,
            d_b_proj,
            d_c_carry + d_c_local,
            d_steps,
            d_la_carry + d_la_local + d_decays[None, :],
        )
        d_extended, d_dtraw, d_cweight, d_cbias, d_dtbias, d_alog = input_back(d_inputs)
        returned = shifted(d_extended[: CONV - 1], "seq", -1)
        d_conv = d_extended[CONV - 1 :] + jnp.pad(returned, ((row_count - (CONV - 1), 0), (0, 0)))
        d_gate_b = d_gate.astype(jnp.bfloat16)
        d_x_b = d_conv[:, :inner].astype(jnp.bfloat16)
        d_shared = d_conv[:, inner:]
        d_dt_b = d_dtraw.astype(jnp.bfloat16)
        d_wz = contract_first(normed, d_gate_b)
        d_wx = contract_first(normed, d_x_b)
        d_wdt = contract_first(normed, d_dt_b)
        d_wbc = lax.dot_general(
            normed.astype(jnp.float32), d_shared, (((0,), (0,)), ((), ())), precision=highest
        )
        wz_now = w_z[layer_idx]
        wx_now = w_x[layer_idx]
        wdt_now = w_dt[layer_idx]
        wbc_now = w_bc[layer_idx]

        def product(weight, grads):
            return lax.dot_general(
                weight, grads, (((1,), (1,)), ((), ())), preferred_element_type=jnp.float32
            )

        shared_rows = wbc_now.astype(jnp.float32)
        shared_term = lax.dot_general(
            shared_rows, d_shared, (((1,), (1,)), ((), ())), precision=highest
        )
        d_normed = lax.psum_scatter(
            product(wz_now, d_gate_b)
            + product(wx_now, d_x_b)
            + product(wdt_now, d_dt_b)
            + shared_term,
            "head",
            scatter_dimension=0,
            tiled=True,
        ).T
        centered = layer_input * factor[:, None]
        d_ngain = jnp.sum(d_normed * centered, axis=0)
        d_unit = d_normed * norm_gain[layer_idx][None, :]
        along_in = token_sums(jnp.sum(d_unit * centered, axis=1)) / D
        grad = grad + factor[:, None] * (d_unit - centered * along_in[:, None])
        weight_sums = (d_wz, d_wx, d_wdt, d_cols, d_wbc)
        maps = jnp.concatenate([d_cweight[:, inner:].reshape(-1), d_cbias[inner:]])
        vectors = (
            d_ngain,
            d_cweight[:, :inner].reshape(-1),
            d_cbias[:inner],
            d_ggain,
            d_dtbias,
            d_alog,
            d_skipped,
        )
        collected[layer_idx] = (weight_sums, vectors, maps)
    sizes = [piece.shape[0] for piece in collected[0][1]]
    maps = lax.psum(jnp.concatenate([entry[2] for entry in collected]), "head")
    own = jnp.concatenate([piece for entry in collected for piece in entry[1]])
    flat = lax.psum(jnp.concatenate([own, maps]), "seq")
    maps = flat[own.shape[0] :].reshape(LAYERS, CONV + 1, -1)
    flat = flat[: own.shape[0]].reshape(LAYERS, -1)
    spots = [sum(sizes[:place]) for place in range(len(sizes) + 1)]
    ngain, cw, cb, ggain, dtb, alog, skipped = [
        flat[:, spots[place] : spots[place + 1]] for place in range(len(sizes))
    ]

    def layers(member, dimension):
        stack = jnp.stack([entry[0][member] for entry in collected]).astype(jnp.bfloat16)
        return lax.psum_scatter(stack, "seq", scatter_dimension=dimension, tiled=True)

    shared = lax.psum(layers(4, 1).astype(jnp.float32), "head")
    shared = lax.all_gather(shared.astype(jnp.bfloat16), "seq", axis=1, tiled=True)

    return (
        hidden,
        grad,
        ngain,
        layers(0, 1).astype(jnp.float32),
        layers(1, 1).astype(jnp.float32),
        shared.astype(jnp.float32),
        layers(2, 1).astype(jnp.float32),
        cw.reshape(LAYERS, CONV, inner),
        cb,
        maps[:, :CONV],
        maps[:, CONV],
        dtb,
        alog,
        skipped,
        ggain,
        layers(3, 2).astype(jnp.float32),
    )


def solution(mesh):
    return jax.shard_map(
        local,
        mesh=mesh,
        in_specs=(
            P("seq", "head"),
            P(None, "head"),
            P(None, None, "head"),
            P(None, None, "head"),
            P(),
            P(None, None, "head"),
            P(None, None, "head"),
            P(None, "head"),
            P(),
            P(),
            P(None, "head"),
            P(None, "head"),
            P(None, "head"),
            P(None, "head"),
            P(None, "head", None),
            P("seq", "head"),
        ),
        out_specs=(
            P("seq", "head"),
            P("seq", "head"),
            P(None, "head"),
            P(None, "seq", "head"),
            P(None, "seq", "head"),
            P(),
            P(None, "seq", "head"),
            P(None, None, "head"),
            P(None, "head"),
            P(),
            P(),
            P(None, "head"),
            P(None, "head"),
            P(None, "head"),
            P(None, "head"),
            P(None, "head", "seq"),
        ),
        check_vma=False,
    )
```
